32 devices in a mesh: param: 16 (over z, y, core), tm: 2 (over x).
Axes of the slice: x: 2, y: 2, z: 4, core: 2. Of those that a mesh axis runs over, the one named last changes fastest.
Arguments:
- params: bfloat16 [32, 32, 8192], P(None, 'tm', 'param'), may hold values from -6 to 6
- kernel: bfloat16 [8, 8192, 600], P(None, 'param'), may hold values from -0.0234375 to 0.0234375
- lag_offsets: int32 [8], replicated, may hold values from 0 to 11, as said below
- observed: bfloat16 [32, 32, 600], P(None, 'tm'), may hold values from -6 to 6
- diag_inverse: float32 [600, 600], replicated, may hold values from -2 to 2, as said below
- coupling: float32 [3, 600, 600], replicated, may hold values from -26 to 26
Outputs:
- whitened: float32 [32, 32, 600], P(None, 'tm')
The draws below stay inside these ranges and needn't reach their ends.
Inputs may be any that keep to these rules, and one draw needn't show every extreme that they name: `lag_offsets`: the offsets are distinct and one of them is always 12 - 1. `diag_inverse`: lower triangular with a positive diagonal.
All inputs are finite; a program needn't handle non-finite values.
Results may differ from the reference program's by a relative error of at most 0.0003.
Values may be sent and summed in bfloat16 or wider, within the bound.
A program may use at most 64 MiB of HBM per device.

```python
import math
import jax
import jax.numpy as jnp
from jax import lax

SENSORS = 600
LAGS = 8
REACH = 12
BAND = 4
SAMPLES = 32
PCOLS = 8192
STEPS = 32


def draw_lag_offsets(key, part):
    chosen = jax.random.permutation(key, REACH - 1)[:LAGS - 1]
    return jnp.concatenate([chosen, jnp.array([REACH - 1])]).astype(jnp.int32)


def noise_parts(key):
    keys = jax.random.split(jax.random.fold_in(key, 7), 4)
    count = SENSORS
    scales = jax.random.uniform(keys[0], (count,), jnp.float32, 0.05, 0.1)
    lower = jax.random.normal(keys[1], (count, count), jnp.float32) * (0.4 * 0.075 / count ** 0.5)
    rate_log = jax.random.uniform(keys[2], (count,), jnp.float32, math.log(0.5 / STEPS), math.log(1.0 / 15.0))
    retention = jnp.exp(-jnp.exp(rate_log))
    inverse_block = jnp.tril(lower, -1) + jnp.diag(scales)
    factor = jnp.linalg.solve(inverse_block, jnp.eye(count, dtype=jnp.float32))
    mixing = jax.random.normal(keys[3], (BAND - 1, count, count), jnp.float32) * (0.0025 / count ** 0.5)
    leading = mixing[0] - jnp.diag(retention)
    stacked = jnp.concatenate([leading[None], mixing[1:]], axis=0)
    coupled = jnp.einsum('mn,jnk->jmk', factor, stacked, precision=lax.Precision.HIGHEST)
    return (inverse_block.astype(jnp.float32), coupled.astype(jnp.float32))


def draw_diag_inverse(key, part):
    inverse_block, coupled = noise_parts(key)
    return inverse_block


def draw_coupling(key, part):
    inverse_block, coupled = noise_parts(key)
    return coupled


def shard_levels(rng, dims, shards, low, largest):
    gain, own = 1.0, jax.random.fold_in(rng, 6)
    for position, shards_of in shards:
        draws = jnp.exp(jax.random.uniform(jax.random.fold_in(own, position), (shards_of,), jnp.float32, low / len(shards), largest / len(shards)))
        gain = gain * jnp.repeat(draws, dims[position] // shards_of).reshape([-1 if axis == position else 1 for axis in range(len(dims))])
    return gain


def gaussian(own_key, extent, scale, reach, pieces=(), held_as=jnp.bfloat16):
    values = scale * jax.random.normal(own_key, extent, jnp.float32)
    if pieces:
        values = values * shard_levels(own_key, extent, pieces, -0.22, 0.18)
    return jnp.clip(values, -reach, reach).astype(held_as)


def setup_inputs(seed: int = 0) -> dict:
    splits = jax.random.split(jax.random.key(seed), 7)
    return {
        "params": gaussian(splits[0], (SAMPLES, STEPS, PCOLS), 1.0, 6.0, ((1, 2), (2, 16))),
        "kernel": gaussian(splits[1], (LAGS, PCOLS, SENSORS), (LAGS * PCOLS) ** -0.5, 0.0234375, ((1, 16),)),
        "lag_offsets": draw_lag_offsets(jax.random.fold_in(splits[6], 71), 0),
        "observed": gaussian(splits[3], (SAMPLES, STEPS, SENSORS), 1.0, 6.0, ((1, 2),)),
        "diag_inverse": draw_diag_inverse(jax.random.fold_in(splits[6], 71), 0),
        "coupling": draw_coupling(jax.random.fold_in(splits[6], 71), 0),
    }


def reference(params, kernel, lag_offsets, observed, diag_inverse, coupling):
    padded = jnp.pad(params, ((0, 0), (REACH - 1, 0), (0, 0)))
    predicted = jnp.zeros((SAMPLES, STEPS, SENSORS), jnp.float32)
    for lag_index in range(LAGS):
        start = (REACH - 1 - lag_offsets[lag_index]).astype(jnp.int32)
        window = lax.dynamic_slice_in_dim(padded, start, STEPS, 1)
        term = jnp.dot(window.reshape(SAMPLES * STEPS, PCOLS).astype(jnp.float32), kernel[lag_index].astype(jnp.float32), preferred_element_type=jnp.float32)
        predicted = predicted + term.reshape(SAMPLES, STEPS, SENSORS)
    misfit = observed.astype(jnp.float32) - predicted

    def advance(history, current):
        balance = current - jnp.einsum('jsn,jmn->sm', history, coupling, precision=lax.Precision.HIGHEST)
        solved = jnp.dot(balance, diag_inverse.T, precision=lax.Precision.HIGHEST)
        history = jnp.concatenate([solved[None], history[:-1]], axis=0)
        return (history, solved)
    start_history = jnp.zeros((BAND - 1, SAMPLES, SENSORS), jnp.float32)
    final_history, solved_all = lax.scan(advance, start_history, jnp.swapaxes(misfit, 0, 1))
    return jnp.swapaxes(solved_all, 0, 1)
```

```python
import functools
import jax
import jax.numpy as jnp
from jax import lax
from jax.experimental import pallas as pl
from jax.experimental.pallas import tpu as pltpu
from jax.sharding import PartitionSpec as P

REACH = 12
LANES = 128
ROWS = 8


def from_behind(block, axis, distance):
    devices = range(lax.axis_size(axis))
    route = [(i - distance, i) for i in devices if i - distance in devices]
    return lax.ppermute(block, axis, route)


def halves(value):
    high = value.astype(jnp.bfloat16).astype(jnp.float32)
    return jnp.concatenate([high, value - high], axis=0).astype(jnp.bfloat16)


def chain_kernel(band, base_ref, weights_ref, out_ref):
    steps, rows, width = base_ref.shape

    def advance(step, past):
        product = jnp.dot(
            jnp.concatenate(past, axis=-1), weights_ref[...], preferred_element_type=jnp.float32
        )
        solved = base_ref[step] - (
            product[:rows, :width] + product[rows:, :width] + product[:rows, width:]
        )
        out_ref[step] = solved
        return (halves(solved),) + past[:-1]

    nothing = halves(base_ref[0] * 0.0)
    lax.fori_loop(0, steps, advance, (nothing,) * band)


def per_device(params, kernel, lag_offsets, observed, diag_inverse, coupling):
    samples, step_count, col_count = params.shape
    lag_count, unused_cols, sensors = kernel.shape
    band = coupling.shape[0]
    width = -(-sensors // LANES) * LANES
    extra = width - sensors
    flat_kernel = kernel.reshape(lag_count * col_count, sensors)
    rim = from_behind(params[:, step_count - (REACH - 1) :, :], "tm", 1)
    source = jnp.concatenate([rim, params], axis=1)
    windows = [
        lax.dynamic_slice_in_dim(source, REACH - 1 - lag_offsets[lag_index], step_count, 1)
        for lag_index in range(lag_count)
    ]
    stacked = jnp.stack(windows, axis=2).reshape(samples * step_count, lag_count * col_count)
    product = jnp.dot(stacked, flat_kernel, preferred_element_type=jnp.float32)
    local = product.reshape(samples, step_count, sensors)
    summed = lax.psum_scatter(local, "param", scatter_dimension=0, tiled=True)
    share = summed.shape[0]
    mine = lax.dynamic_slice_in_dim(observed, lax.axis_index("param") * share, share, 0)
    misfit = mine.astype(jnp.float32) - summed

    weights = jnp.einsum("jkn,mk->jnm", coupling, diag_inverse, precision=lax.Precision.HIGHEST)
    weights = jnp.pad(weights, ((0, 0), (0, extra), (0, extra))).reshape(band * width, width)
    high = lax.reduce_precision(weights, 8, 7)
    pair = jnp.concatenate([high, weights - high], axis=-1).astype(jnp.bfloat16)

    base = jnp.dot(misfit, diag_inverse.T, precision=lax.Precision.HIGHEST)
    base = lax.all_gather(base, "tm", axis=1, tiled=True)
    total = base.shape[1]
    base = jnp.pad(jnp.swapaxes(base, 0, 1), ((0, 0), (0, ROWS - share), (0, extra)))
    solved = pl.pallas_call(
        functools.partial(chain_kernel, band),
        out_shape=jax.ShapeDtypeStruct((total, ROWS, width), jnp.float32),
        in_specs=[pl.BlockSpec(memory_space=pltpu.VMEM)] * 2,
        out_specs=pl.BlockSpec(memory_space=pltpu.VMEM),
    )(base, pair)
    own = lax.dynamic_slice_in_dim(solved, lax.axis_index("tm") * step_count, step_count, 0)
    outputs = jnp.swapaxes(own[:, :share, :sensors], 0, 1)
    return lax.all_gather(outputs, "param", axis=0, tiled=True)


def solution(mesh):
    in_specs = (P(None, "tm", "param"), P(None, "param", None), P(), P(None, "tm", None), P(), P())
    out_specs = P(None, "tm", None)
    return jax.shard_map(
        per_device, mesh=mesh, in_specs=in_specs, out_specs=out_specs, check_vma=False
    )
```

```python
import functools
import jax
import jax.numpy as jnp
from jax import lax
from jax.experimental import pallas as pl
from jax.experimental.pallas import tpu as pltpu
from jax.sharding import PartitionSpec as P

REACH = 12
LANES = 128
ROWS = 8


def from_behind(block, axis, distance):
    devices = range(lax.axis_size(axis))
    route = [(i - distance, i) for i in devices if i - distance in devices]
    return lax.ppermute(block, axis, route)


def halves(value):
    high = value.astype(jnp.bfloat16).astype(jnp.float32)
    return jnp.concatenate([high, value - high], axis=0).astype(jnp.bfloat16)


def chain_kernel(band, base_ref, weights_ref, out_ref):
    steps, rows, width = base_ref.shape

    def advance(step, past):
        product = jnp.dot(
            jnp.concatenate(past, axis=-1), weights_ref[...], preferred_element_type=jnp.float32
        )
        solved = base_ref[step] - (
            product[:rows, :width] + product[rows:, :width] + product[:rows, width:]
        )
        out_ref[step] = solved
        return (halves(solved),) + past[:-1]

    nothing = halves(base_ref[0] * 0.0)
    lax.fori_loop(0, steps, advance, (nothing,) * band)


MESH = pl.DeviceIdType.MESH


def place():
    me = lax.axis_index("param")
    return lax.div(me, 2), lax.rem(me, 2), lax.axis_size("param") // 2


def greet(chip, core, chips):
    barrier = pltpu.get_barrier_semaphore()
    others = [2 * chip + 1 - core]
    others += [2 * lax.rem(chip + k, chips) + core for k in range(1, chips)]
    for other in others:
        pl.semaphore_signal(barrier, inc=1, device_id={"param": other}, device_id_type=MESH)
    pl.semaphore_wait(barrier, chips)


def send(source, target, send_sem, recv_sem, other):
    copy = pltpu.make_async_remote_copy(
        src_ref=source,
        dst_ref=target,
        send_sem=send_sem,
        recv_sem=recv_sem,
        device_id={"param": other},
        device_id_type=MESH,
    )
    copy.start()
    return copy


def reduce_kernel(
    local_ref, out_ref, pair_in, partial, landed, pair_send, pair_recv, chip_send, chip_recv
):
    chip, core, chips = place()
    greet(chip, core, chips)
    turns = [lax.rem(chip + k, chips) for k in range(1, chips + 1)]
    pairs = [
        send(local_ref.at[q, 1 - core], pair_in.at[k], pair_send.at[k], pair_recv.at[k], 2 * chip + 1 - core)
        for k, q in enumerate(turns)
    ]
    sends = []
    for k, q in enumerate(turns):
        pairs[k].wait_recv()
        if k < chips - 1:
            partial[k] = local_ref[q, core] + pair_in[k]
            sends.append(
                send(partial.at[k], landed.at[k], chip_send.at[k], chip_recv.at[k], 2 * q + core)
            )
        else:
            total = local_ref[q, core] + pair_in[k]
    for k in range(chips - 1):
        sends[k].wait_recv()
        total = total + landed[k]
    out_ref[...] = total
    for copy in pairs + sends:
        copy.wait_send()


def gather_kernel(own_ref, out_ref, pair_send, pair_recv, chip_send, chip_recv):
    chip, core, chips = place()
    greet(chip, core, chips)
    other = 2 * chip + 1 - core
    sends = [
        send(own_ref, out_ref.at[chip, core], chip_send.at[k - 1], chip_recv.at[k - 1], 2 * lax.rem(chip + k, chips) + core)
        for k in range(1, chips)
    ]
    pairs = [send(own_ref, out_ref.at[chip, core], pair_send.at[0], pair_recv.at[0], other)]
    out_ref[chip, core] = own_ref[...]
    for k in range(1, chips):
        sends[k - 1].wait_recv()
        block = out_ref.at[lax.rem(chip - k + chips, chips), core]
        pairs.append(send(block, block, pair_send.at[k], pair_recv.at[k], other))
    for copy in pairs:
        copy.wait_recv()
    for copy in pairs + sends:
        copy.wait_send()


def reduce_scatter(local):
    chips = lax.axis_size("param") // 2
    share = local.shape[0] // (2 * chips)
    block = (share,) + local.shape[1:]
    return pl.pallas_call(
        reduce_kernel,
        out_shape=jax.ShapeDtypeStruct(block, jnp.float32),
        in_specs=[pl.BlockSpec(memory_space=pltpu.VMEM)],
        out_specs=pl.BlockSpec(memory_space=pltpu.VMEM),
        scratch_shapes=[
            pltpu.VMEM((chips,) + block, jnp.float32),
            pltpu.VMEM((chips - 1,) + block, jnp.float32),
            pltpu.VMEM((chips - 1,) + block, jnp.float32),
            pltpu.SemaphoreType.DMA((chips,)),
            pltpu.SemaphoreType.DMA((chips,)),
            pltpu.SemaphoreType.DMA((chips - 1,)),
            pltpu.SemaphoreType.DMA((chips - 1,)),
        ],
        compiler_params=pltpu.CompilerParams(collective_id=0, has_side_effects=True),
    )(local.reshape((chips, 2) + block))


def gather(own):
    chips = lax.axis_size("param") // 2
    whole = pl.pallas_call(
        gather_kernel,
        out_shape=jax.ShapeDtypeStruct((chips, 2) + own.shape, jnp.float32),
        in_specs=[pl.BlockSpec(memory_space=pltpu.VMEM)],
        out_specs=pl.BlockSpec(memory_space=pltpu.VMEM),
        scratch_shapes=[
            pltpu.SemaphoreType.DMA((chips,)),
            pltpu.SemaphoreType.DMA((chips,)),
            pltpu.SemaphoreType.DMA((chips - 1,)),
            pltpu.SemaphoreType.DMA((chips - 1,)),
        ],
        compiler_params=pltpu.CompilerParams(collective_id=1, has_side_effects=True),
    )(own)
    return whole.reshape((2 * chips * own.shape[0],) + own.shape[1:])


def per_device(params, kernel, lag_offsets, observed, diag_inverse, coupling):
    samples, step_count, col_count = params.shape
    lag_count, unused_cols, sensors = kernel.shape
    band = coupling.shape[0]
    width = -(-sensors // LANES) * LANES
    extra = width - sensors
    flat_kernel = kernel.reshape(lag_count * col_count, sensors)
    rim = from_behind(params[:, step_count - (REACH - 1) :, :], "tm", 1)
    source = jnp.concatenate([rim, params], axis=1)
    windows = [
        lax.dynamic_slice_in_dim(source, REACH - 1 - lag_offsets[lag_index], step_count, 1)
        for lag_index in range(lag_count)
    ]
    stacked = jnp.stack(windows, axis=2).reshape(samples * step_count, lag_count * col_count)
    product = jnp.dot(stacked, flat_kernel, preferred_element_type=jnp.float32)
    local = product.reshape(samples, step_count, sensors)
    summed = reduce_scatter(local)
    share = summed.shape[0]
    mine = lax.dynamic_slice_in_dim(observed, lax.axis_index("param") * share, share, 0)
    misfit = mine.astype(jnp.float32) - summed

    coupling_high = lax.reduce_precision(coupling, 8, 7)
    inverse_high = lax.reduce_precision(diag_inverse, 8, 7)
    weights = jnp.einsum(
        "jkn,mk->jnm",
        jnp.concatenate([coupling_high, coupling - coupling_high, coupling_high], axis=1).astype(jnp.bfloat16),
        jnp.concatenate([inverse_high, inverse_high, diag_inverse - inverse_high], axis=1).astype(jnp.bfloat16),
        preferred_element_type=jnp.float32,
    )
    weights = jnp.pad(weights, ((0, 0), (0, extra), (0, extra))).reshape(band * width, width)
    high = lax.reduce_precision(weights, 8, 7)
    pair = jnp.concatenate([high, weights - high], axis=-1).astype(jnp.bfloat16)

    base = jnp.dot(misfit, diag_inverse.T, precision=lax.Precision.HIGHEST)
    base = lax.all_gather(base, "tm", axis=1, tiled=True)
    total = base.shape[1]
    base = jnp.pad(jnp.swapaxes(base, 0, 1), ((0, 0), (0, ROWS - share), (0, extra)))
    solved = pl.pallas_call(
        functools.partial(chain_kernel, band),
        out_shape=jax.ShapeDtypeStruct((total, ROWS, width), jnp.float32),
        in_specs=[pl.BlockSpec(memory_space=pltpu.VMEM)] * 2,
        out_specs=pl.BlockSpec(memory_space=pltpu.VMEM),
    )(base, pair)
    own = lax.dynamic_slice_in_dim(solved, lax.axis_index("tm") * step_count, step_count, 0)
    outputs = jnp.swapaxes(own[:, :share, :sensors], 0, 1)
    return gather(outputs)


def solution(mesh):
    in_specs = (P(None, "tm", "param"), P(None, "param", None), P(), P(None, "tm", None), P(), P())
    out_specs = P(None, "tm", None)
    return jax.shard_map(
        per_device, mesh=mesh, in_specs=in_specs, out_specs=out_specs, check_vma=False
    )
```

```python
import functools
import jax
import jax.numpy as jnp
from jax import lax
from jax.experimental import pallas as pl
from jax.experimental.pallas import tpu as pltpu
from jax.sharding import PartitionSpec as P

REACH = 12
LANES = 128
ROWS = 8


def from_behind(block, axis, distance):
    devices = range(lax.axis_size(axis))
    route = [(i - distance, i) for i in devices if i - distance in devices]
    return lax.ppermute(block, axis, route)


def halves(value):
    high = value.astype(jnp.bfloat16).astype(jnp.float32)
    return jnp.concatenate([high, value - high], axis=0).astype(jnp.bfloat16)


def chain_kernel(band, base_ref, weights_ref, out_ref):
    steps, rows, width = base_ref.shape

    def advance(step, past):
        product = jnp.dot(
            jnp.concatenate(past, axis=-1), weights_ref[...], preferred_element_type=jnp.float32
        )
        solved = base_ref[step] - (
            product[:rows, :width] + product[rows:, :width] + product[:rows, width:]
        )
        out_ref[step] = solved
        return (halves(solved),) + past[:-1]

    nothing = halves(base_ref[0] * 0.0)
    lax.fori_loop(0, steps, advance, (nothing,) * band)


MESH = pl.DeviceIdType.MESH


def place():
    me = lax.axis_index("param")
    return lax.div(me, 2), lax.rem(me, 2), lax.axis_size("param") // 2


def greet(chip, core, chips):
    barrier = pltpu.get_barrier_semaphore()
    others = [2 * chip + 1 - core]
    others += [2 * lax.rem(chip + k, chips) + core for k in range(1, chips)]
    for other in others:
        pl.semaphore_signal(barrier, inc=1, device_id={"param": other}, device_id_type=MESH)
    pl.semaphore_wait(barrier, chips)


def send(source, target, send_sem, recv_sem, other):
    copy = pltpu.make_async_remote_copy(
        src_ref=source,
        dst_ref=target,
        send_sem=send_sem,
        recv_sem=recv_sem,
        device_id={"param": other},
        device_id_type=MESH,
    )
    copy.start()
    return copy


def reduce_kernel(
    local_ref, out_ref, pair_in, partial, landed, pair_send, pair_recv, chip_send, chip_recv
):
    chip, core, chips = place()
    greet(chip, core, chips)
    turns = [lax.rem(chip + k, chips) for k in range(1, chips + 1)]
    pairs = [
        send(local_ref.at[q, 1 - core], pair_in.at[k], pair_send.at[k], pair_recv.at[k], 2 * chip + 1 - core)
        for k, q in enumerate(turns)
    ]
    sends = []
    for k, q in enumerate(turns):
        pairs[k].wait_recv()
        if k < chips - 1:
            partial[k] = local_ref[q, core] + pair_in[k]
            sends.append(
                send(partial.at[k], landed.at[k], chip_send.at[k], chip_recv.at[k], 2 * q + core)
            )
        else:
            total = local_ref[q, core] + pair_in[k]
    for k in range(chips - 1):
        sends[k].wait_recv()
        total = total + landed[k]
    out_ref[...] = total
    for copy in pairs + sends:
        copy.wait_send()


def gather_kernel(own_ref, out_ref, pair_send, pair_recv, chip_send, chip_recv):
    chip, core, chips = place()
    greet(chip, core, chips)
    other = 2 * chip + 1 - core
    sends = [
        send(own_ref, out_ref.at[chip, core], chip_send.at[k - 1], chip_recv.at[k - 1], 2 * lax.rem(chip + k, chips) + core)
        for k in range(1, chips)
    ]
    pairs = [send(own_ref, out_ref.at[chip, core], pair_send.at[0], pair_recv.at[0], other)]
    out_ref[chip, core] = own_ref[...]
    for k in range(1, chips):
        sends[k - 1].wait_recv()
        block = out_ref.at[lax.rem(chip - k + chips, chips), core]
        pairs.append(send(block, block, pair_send.at[k], pair_recv.at[k], other))
    for copy in pairs:
        copy.wait_recv()
    for copy in pairs + sends:
        copy.wait_send()


def reduce_scatter(local):
    chips = lax.axis_size("param") // 2
    share = local.shape[0] // (2 * chips)
    block = (share,) + local.shape[1:]
    return pl.pallas_call(
        reduce_kernel,
        out_shape=jax.ShapeDtypeStruct(block, jnp.float32),
        in_specs=[pl.BlockSpec(memory_space=pltpu.VMEM)],
        out_specs=pl.BlockSpec(memory_space=pltpu.VMEM),
        scratch_shapes=[
            pltpu.VMEM((chips,) + block, jnp.float32),
            pltpu.VMEM((chips - 1,) + block, jnp.float32),
            pltpu.VMEM((chips - 1,) + block, jnp.float32),
            pltpu.SemaphoreType.DMA((chips,)),
            pltpu.SemaphoreType.DMA((chips,)),
            pltpu.SemaphoreType.DMA((chips - 1,)),
            pltpu.SemaphoreType.DMA((chips - 1,)),
        ],
        compiler_params=pltpu.CompilerParams(collective_id=0, has_side_effects=True),
    )(local.reshape((chips, 2) + block))


def gather(own):
    chips = lax.axis_size("param") // 2
    whole = pl.pallas_call(
        gather_kernel,
        out_shape=jax.ShapeDtypeStruct((chips, 2) + own.shape, jnp.float32),
        in_specs=[pl.BlockSpec(memory_space=pltpu.VMEM)],
        out_specs=pl.BlockSpec(memory_space=pltpu.VMEM),
        scratch_shapes=[
            pltpu.SemaphoreType.DMA((chips,)),
            pltpu.SemaphoreType.DMA((chips,)),
            pltpu.SemaphoreType.DMA((chips - 1,)),
            pltpu.SemaphoreType.DMA((chips - 1,)),
        ],
        compiler_params=pltpu.CompilerParams(collective_id=1, has_side_effects=True),
    )(own)
    return whole.reshape((2 * chips * own.shape[0],) + own.shape[1:])


def per_device(params, kernel, lag_offsets, observed, diag_inverse, coupling):
    samples, step_count, col_count = params.shape
    lag_count, unused_cols, sensors = kernel.shape
    band = coupling.shape[0]
    width = -(-sensors // LANES) * LANES
    extra = width - sensors
    flat_kernel = kernel.reshape(lag_count * col_count, sensors)
    rim = from_behind(params[:, step_count - (REACH - 1) :, :], "tm", 1)
    source = jnp.concatenate([rim, params], axis=1)
    windows = [
        lax.dynamic_slice_in_dim(source, REACH - 1 - lag_offsets[lag_index], step_count, 1)
        for lag_index in range(lag_count)
    ]
    stacked = jnp.stack(windows, axis=2).reshape(samples * step_count, lag_count * col_count)
    product = jnp.dot(stacked, flat_kernel, preferred_element_type=jnp.float32)
    local = product.reshape(samples, step_count, sensors)
    summed = reduce_scatter(local)
    share = summed.shape[0]
    mine = lax.dynamic_slice_in_dim(observed, lax.axis_index("param") * share, share, 0)
    misfit = mine.astype(jnp.float32) - summed

    weights = jnp.einsum("jkn,mk->jnm", coupling, diag_inverse, precision=lax.Precision.HIGH)
    weights = jnp.pad(weights, ((0, 0), (0, extra), (0, extra))).reshape(band * width, width)
    high = lax.reduce_precision(weights, 8, 7)
    pair = jnp.concatenate([high, weights - high], axis=-1).astype(jnp.bfloat16)

    base = jnp.dot(misfit, diag_inverse.T, precision=lax.Precision.HIGHEST)
    base = lax.all_gather(base, "tm", axis=1, tiled=True)
    total = base.shape[1]
    base = jnp.pad(jnp.swapaxes(base, 0, 1), ((0, 0), (0, ROWS - share), (0, extra)))
    solved = pl.pallas_call(
        functools.partial(chain_kernel, band),
        out_shape=jax.ShapeDtypeStruct((total, ROWS, width), jnp.float32),
        in_specs=[pl.BlockSpec(memory_space=pltpu.VMEM)] * 2,
        out_specs=pl.BlockSpec(memory_space=pltpu.VMEM),
    )(base, pair)
    own = lax.dynamic_slice_in_dim(solved, lax.axis_index("tm") * step_count, step_count, 0)
    outputs = jnp.swapaxes(own[:, :share, :sensors], 0, 1)
    return gather(outputs)


def solution(mesh):
    in_specs = (P(None, "tm", "param"), P(None, "param", None), P(), P(None, "tm", None), P(), P())
    out_specs = P(None, "tm", None)
    return jax.shard_map(
        per_device, mesh=mesh, in_specs=in_specs, out_specs=out_specs, check_vma=False
    )
```
